32 devices in a mesh: tm: 8 (over y, x, core), rows: 4 (over z).
Axes of the slice: x: 2, y: 2, z: 4, core: 2. Of those that a mesh axis runs over, the one named last changes fastest.
Arguments:
- video: bfloat16 [16, 16, 120, 128], P('tm', 'rows'), may hold values from -6 to 6
- norm_gain: bfloat16 [128], replicated, may hold values from 0.099609375 to 1.8984375
- conv_first: bfloat16 [3, 3, 3, 128, 128], replicated, may hold values from -0.109375 to 0.109375
- conv_second: bfloat16 [3, 3, 3, 128, 128], replicated, may hold values from -0.109375 to 0.109375
- attn_gain: bfloat16 [128], replicated, may hold values from 0.099609375 to 1.8984375
- query_weight: bfloat16 [128, 128], replicated, may hold values from -2 to 2
- key_weight: bfloat16 [128, 128], replicated, may hold values from -2 to 2
- value_weight: bfloat16 [128, 128], replicated, may hold values from -0.5 to 0.5
- out_weight: bfloat16 [128, 128], replicated, may hold values from -0.5 to 0.5
Outputs:
- result: bfloat16 [16, 16, 120, 128], P('tm', 'rows')
The draws below stay inside these ranges and needn't reach their ends.
All inputs are finite; a program needn't handle non-finite values.
Results may differ from the reference program's by a relative error of at most 0.013.
Values may be sent and summed in bfloat16 or wider, within the bound.
No kernel may reach another device: no remote copies, remote signals or barrier semaphores. Data moves between devices by JAX's collectives and lax.ppermute only.
A program may use at most 64 MiB of HBM per device.

```python
import jax
import jax.numpy as jnp
from jax import lax

C = 128
W = 120
FRAMES = 16
HEIGHT = 16


def shared_base(key):
    return jnp.clip(jax.random.normal(jax.random.fold_in(key, 11), (C, C), jnp.float32), -4.0, 4.0)


def draw_query_weight(key, part):
    base = shared_base(key)
    scaled = base * C ** (-0.5)
    return jnp.clip(scaled, -2.0, 2.0).astype(jnp.bfloat16)


def draw_key_weight(key, part):
    other = jnp.clip(jax.random.normal(jax.random.fold_in(key, 13), (C, C), jnp.float32), -4.0, 4.0)
    scaled = other * C ** (-0.5)
    return jnp.clip(scaled, -2.0, 2.0).astype(jnp.bfloat16)


def block_scale(stream_key, extent, cuts, least, largest):
    level, own = 1.0, jax.random.fold_in(stream_key, 6)
    for dim, blocks in cuts:
        draws = jnp.exp(jax.random.uniform(jax.random.fold_in(own, dim), (blocks,), jnp.float32, least / len(cuts), largest / len(cuts)))
        level = level * jnp.repeat(draws, extent[dim] // blocks).reshape([-1 if axis == dim else 1 for axis in range(len(extent))])
    return level


def gaussian(own_key, shape, scale, limit, shards=(), held_as=jnp.bfloat16):
    entries = scale * jax.random.normal(own_key, shape, jnp.float32)
    if shards:
        entries = entries * block_scale(own_key, shape, shards, -0.22, 0.18)
    return jnp.clip(entries, -limit, limit).astype(held_as)


def setup_inputs(seed: int = 0) -> dict:
    arg_keys = jax.random.split(jax.random.key(seed), 10)
    video = gaussian(arg_keys[0], (FRAMES, HEIGHT, W, C), 1.0, 6.0, ((0, 8), (1, 4)))
    norm_gain = jnp.clip(1.0 + 0.18 * jax.random.normal(arg_keys[1], (C,), jnp.float32), 0.099609375, 1.8984375).astype(jnp.bfloat16)
    conv_first = gaussian(arg_keys[2], (3, 3, 3, C, C), (27 * C) ** -0.5, 0.109375)
    conv_second = gaussian(arg_keys[3], (3, 3, 3, C, C), (27 * C) ** -0.5, 0.109375)
    attn_gain = jnp.clip(1.0 + 0.18 * jax.random.normal(arg_keys[4], (C,), jnp.float32), 0.099609375, 1.8984375).astype(jnp.bfloat16)
    query_weight = draw_query_weight(jax.random.fold_in(arg_keys[9], 71), 0)
    key_weight = draw_key_weight(jax.random.fold_in(arg_keys[9], 71), 0)
    value_weight = gaussian(arg_keys[7], (C, C), C ** -0.5, 0.5)
    out_weight = gaussian(arg_keys[8], (C, C), C ** -0.5, 0.5)
    return {"video": video, "norm_gain": norm_gain, "conv_first": conv_first, "conv_second": conv_second, "attn_gain": attn_gain, "query_weight": query_weight, "key_weight": key_weight, "value_weight": value_weight, "out_weight": out_weight}


def rms_norm(values, gain):
    wide = values.astype(jnp.float32)
    scale = lax.rsqrt(lax.optimization_barrier(jnp.mean(wide * wide, axis=-1, keepdims=True)) + 1e-06)
    return wide * scale * gain.astype(jnp.float32)

def conv_taps(padded, kernel, frames, height, width):
    chans = kernel.shape[-1]
    total = jnp.zeros((frames * height * width, chans), jnp.float32)
    for shift_t in range(3):
        for shift_h in range(3):
            slab = padded[shift_t:shift_t + frames, shift_h:shift_h + height]
            joined = jnp.concatenate([slab[:, :, e:e + width] for e in range(3)], axis=-1)
            taps = kernel[shift_t, shift_h].reshape(3 * chans, chans)
            total = total + jnp.dot(joined.reshape(-1, 3 * chans), taps, preferred_element_type=jnp.float32)
    return total.reshape(frames, height, width, chans)

def convolve(field, kernel):
    frames, height, width, chans = field.shape
    padded = jnp.pad(field, ((2, 0), (1, 1), (1, 1), (0, 0)))
    return conv_taps(padded, kernel, frames, height, width)

def reference(video, norm_gain, conv_first, conv_second, attn_gain, query_weight, key_weight, value_weight, out_weight):
    frames, height, width, chans = video.shape
    act = jax.nn.silu(rms_norm(video, norm_gain)).astype(jnp.bfloat16)
    mid = jax.nn.silu(convolve(act, conv_first)).astype(jnp.bfloat16)
    hidden = (video.astype(jnp.float32) + convolve(mid, conv_second)).astype(jnp.bfloat16)
    normed = rms_norm(hidden, attn_gain).astype(jnp.bfloat16)
    flat = normed.reshape(-1, chans)
    query = jnp.dot(flat, query_weight, preferred_element_type=jnp.float32).astype(jnp.bfloat16)
    keys = jnp.dot(flat, key_weight, preferred_element_type=jnp.float32).astype(jnp.bfloat16)
    values = jnp.dot(flat, value_weight, preferred_element_type=jnp.float32).astype(jnp.bfloat16)
    cells = height * width
    query = query.reshape(frames, cells, chans).astype(jnp.float32)
    keys = keys.reshape(frames, cells, chans).astype(jnp.float32)
    values = values.reshape(frames, cells, chans).astype(jnp.float32)
    scores = jnp.einsum('fpc,gpc->fgp', query, keys) / jnp.sqrt(jnp.float32(chans))
    position = jnp.arange(frames, dtype=jnp.int32)
    allowed = (position[None, :] <= position[:, None])[:, :, None]
    top = lax.optimization_barrier(jnp.max(jnp.where(allowed, scores, jnp.float32(-1e+30)), axis=1))
    weights = jnp.where(allowed, jnp.exp(scores - top[:, None, :]), jnp.float32(0.0))
    total = lax.optimization_barrier(jnp.sum(weights, axis=1))
    acc = jnp.einsum('fgp,gpc->fpc', weights.astype(jnp.bfloat16).astype(jnp.float32), values)
    mixed = (acc / total[:, :, None]).astype(jnp.bfloat16)
    projected = jnp.dot(mixed.reshape(-1, chans), out_weight, preferred_element_type=jnp.float32)
    result = hidden.reshape(-1, chans).astype(jnp.float32) + projected
    return result.astype(jnp.bfloat16).reshape(frames, height, width, chans)
```

```python
import functools

import jax
import jax.numpy as jnp
from jax import lax
from jax.experimental import pallas as pl
from jax.experimental.pallas import tpu as pltpu
from jax.sharding import PartitionSpec as P

F32 = jnp.float32
BF16 = jnp.bfloat16
EPS = 1e-06


def round_up(n, m):
    return (n + m - 1) // m * m


def silu(v):
    return v / (1.0 + jnp.exp(-v))


def rms(v, gain):
    scale = lax.rsqrt(jnp.mean(v * v, axis=-1, keepdims=True) + EPS)
    return v * scale * gain


def lagged(v, steps):
    frame = lax.broadcasted_iota(jnp.int32, v.shape, 0)
    return jnp.where(frame < steps, 0.0, pltpu.roll(v, steps, 0))


def store_taps(dst, row, col, v):
    chans = v.shape[-1]
    for lag in range(3):
        moved = v if lag == 0 else lagged(v, lag)
        dst[row, col, :, lag * chans : (lag + 1) * chans] = moved.astype(BF16)


def build_pair_weight(dst, src):
    chans = src.shape[-1]
    zero = jnp.zeros((chans, chans), BF16)
    for e in range(3):
        for j in range(4):
            for lag in range(3):
                a = 2 - lag
                rows = slice(lag * chans, (lag + 1) * chans)
                dst[e, j, rows, :chans] = src[a, j, e] if j < 3 else zero
                dst[e, j, rows, chans:] = src[a, j - 1, e] if j > 0 else zero


def pair_conv(field, weight, pairs, cols, frames):
    total = None
    depth = field.shape[-1]
    for e in range(3):
        for j in range(4):
            parts = [
                field[2 * p + j, e : e + cols].reshape(cols * frames, depth) for p in range(pairs)
            ]
            lhs = parts[0] if pairs == 1 else jnp.concatenate(parts, axis=0)
            term = jnp.dot(lhs, weight[e, j], preferred_element_type=F32)
            total = term if total is None else total + term
    return total


def block_kernel(
    width,
    height,
    block,
    own_ref,
    above_ref,
    below_ref,
    gain1_ref,
    k1_ref,
    k2_ref,
    gain2_ref,
    wqkv_ref,
    wo_ref,
    out_ref,
    taps1,
    taps2,
    pw1,
    pw2,
    flat,
    raw,
    kept,
    hid,
    qkv,
    res,
):
    frames, rows, wide, chans = own_ref.shape
    first_col = lax.axis_index("tm") * block
    first_row = lax.axis_index("rows") * rows
    gain1 = gain1_ref[...].astype(F32)
    gain2 = gain2_ref[...].astype(F32)

    build_pair_weight(pw1, k1_ref)
    build_pair_weight(pw2, k2_ref)

    for r in range(rows + 4):
        if r < 2:
            x = above_ref[:, r]
        elif r < rows + 2:
            x = own_ref[:, r - 2]
        else:
            x = below_ref[:, r - rows - 2]
        x = x.astype(F32).reshape(frames * wide, chans)
        flat[...] = silu(rms(x, gain1))
        inner = 2 <= r < rows + 2
        if inner:
            raw[...] = x
        for c in range(block + 4):
            v = flat[pl.ds(c, frames, stride=wide), :]
            store_taps(taps1, r, c, v)
            if inner and 2 <= c < block + 2:
                kept[r - 2, c - 2] = raw[pl.ds(c, frames, stride=wide), :]

    cols = block + 2
    pairs = (rows + 2) // 2
    first = pair_conv(taps1, pw1, pairs, cols, frames)
    first = silu(first)
    for p in range(pairs):
        for c in range(cols):
            at = (p * cols + c) * frames
            col = first_col + (c - 1)
            for k in range(2):
                row = first_row + (2 * p + k - 1)
                inside = (col >= 0) & (col < width) & (row >= 0) & (row < height)
                v = first[at : at + frames, k * chans : (k + 1) * chans]
                store_taps(taps2, 2 * p + k, c, jnp.where(inside, v, 0.0))

    pairs = rows // 2
    second = pair_conv(taps2, pw2, pairs, block, frames)
    for p in range(pairs):
        for c in range(block):
            at = (p * block + c) * frames
            for k in range(2):
                r = 2 * p + k
                v = kept[r, c] + second[at : at + frames, k * chans : (k + 1) * chans]
                to = (r * block + c) * frames
                hid[to : to + frames, :] = v.astype(BF16)

    normed = rms(hid[...].astype(F32), gain2).astype(BF16)
    qkv[...] = jnp.dot(normed, wqkv_ref[...], preferred_element_type=F32).astype(BF16)
    count = rows * block * frames
    step = max(128 // frames, 1) * frames
    scale = 1.0 / (float(chans) ** 0.5)
    for lo in range(0, count, step):
        n = min(step, count - lo)
        query = qkv[lo : lo + n, :chans]
        keys = qkv[lo : lo + n, chans : 2 * chans]
        values = qkv[lo : lo + n, 2 * chans :]
        score = lax.dot_general(
            query, keys, (((1,), (1,)), ((), ())), preferred_element_type=F32
        )
        score = score * scale
        i = lax.broadcasted_iota(jnp.int32, (n, n), 0)
        j = lax.broadcasted_iota(jnp.int32, (n, n), 1)
        allowed = (j <= i) & (j >= i - lax.rem(i, frames))
        top = jnp.max(jnp.where(allowed, score, -1e30), axis=-1, keepdims=True)
        terms = jnp.where(allowed, jnp.exp(score - top), 0.0)
        total = jnp.sum(terms, axis=-1, keepdims=True)
        mixed = jnp.dot(terms.astype(BF16), values, preferred_element_type=F32) / total
        out = jnp.dot(mixed.astype(BF16), wo_ref[...], preferred_element_type=F32)
        res[lo : lo + n, :] = hid[lo : lo + n, :].astype(F32) + out

    wide_out = out_ref.shape[2]
    for r in range(rows):
        for c in range(block):
            at = (r * block + c) * frames
            flat[pl.ds(c, frames, stride=wide_out), :] = res[at : at + frames, :]
        back = flat[0 : frames * wide_out, :]
        out_ref[:, r] = back.reshape(frames, wide_out, chans).astype(BF16)


def local(
    width,
    height,
    video,
    norm_gain,
    conv_first,
    conv_second,
    attn_gain,
    query_weight,
    key_weight,
    value_weight,
    out_weight,
):
    few, rows, _, chans = video.shape
    across = lax.axis_size("tm")
    down = lax.axis_size("rows")
    frames = few * across
    block = (width + across - 1) // across
    wide = round_up(block + 4, 8)
    wide_out = round_up(block, 8)

    right = (across - 1) * block + wide - 2 - width
    padded = jnp.pad(video, ((0, 0), (0, 0), (2, right), (0, 0)))
    sent = jnp.stack([padded[:, :, t * block : t * block + wide] for t in range(across)])
    own = lax.all_to_all(sent, "tm", 0, 0, tiled=True).reshape(frames, rows, wide, chans)

    above = lax.ppermute(own[:, rows - 2 :], "rows", [(i, i + 1) for i in range(down - 1)])
    below = lax.ppermute(own[:, :2], "rows", [(i + 1, i) for i in range(down - 1)])

    wqkv = jnp.concatenate([query_weight, key_weight, value_weight], axis=1)
    count = rows * block * frames
    vmem = pl.BlockSpec(memory_space=pltpu.VMEM)
    out = pl.pallas_call(
        functools.partial(block_kernel, width, height, block),
        out_shape=jax.ShapeDtypeStruct((frames, rows, wide_out, chans), BF16),
        in_specs=[vmem] * 9,
        out_specs=vmem,
        scratch_shapes=[
            pltpu.VMEM((rows + 4, block + 4, frames, 3 * chans), BF16),
            pltpu.VMEM((rows + 2, block + 2, frames, 3 * chans), BF16),
            pltpu.VMEM((3, 4, 3 * chans, 2 * chans), BF16),
            pltpu.VMEM((3, 4, 3 * chans, 2 * chans), BF16),
            pltpu.VMEM((frames * wide, chans), F32),
            pltpu.VMEM((frames * wide, chans), F32),
            pltpu.VMEM((rows, block, frames, chans), F32),
            pltpu.VMEM((count, chans), BF16),
            pltpu.VMEM((count, 3 * chans), BF16),
            pltpu.VMEM((count, chans), F32),
        ],
        compiler_params=pltpu.CompilerParams(vmem_limit_bytes=48 << 20),
        name="block",
    )(
        own,
        above,
        below,
        norm_gain.reshape(1, chans),
        conv_first,
        conv_second,
        attn_gain.reshape(1, chans),
        wqkv,
        out_weight,
    )

    sent = out.reshape(across, few, rows, wide_out, chans)
    got = lax.all_to_all(sent, "tm", 0, 0, tiled=True)[:, :, :, :block]
    got = got.transpose(1, 2, 0, 3, 4).reshape(few, rows, across * block, chans)
    return got[:, :, :width]


def solution(mesh):
    spec = P("tm", "rows", None, None)

    def whole(video, *params):
        fn = functools.partial(local, video.shape[2], video.shape[1])
        return jax.shard_map(
            fn, mesh=mesh, in_specs=(spec,) + (P(),) * 8, out_specs=spec, check_vma=False
        )(video, *params)

    return whole
```

```python
import functools

import jax
import jax.numpy as jnp
from jax import lax
from jax.experimental import pallas as pl
from jax.experimental.pallas import tpu as pltpu
from jax.sharding import PartitionSpec as P

F32 = jnp.float32
BF16 = jnp.bfloat16
EPS = 1e-06
VMEM = pl.BlockSpec(memory_space=pltpu.VMEM)


def round_up(n, m):
    return (n + m - 1) // m * m


def silu(v):
    half = 0.5 * v
    return half + half * jnp.tanh(half)


def rms(v, gain):
    scale = lax.rsqrt(jnp.mean(v * v, axis=-1, keepdims=True) + EPS)
    return v * scale * gain


class Plan:
    def __init__(self, video, across, width, height):
        self.few, self.rows, _, self.chans = video.shape
        self.across, self.width, self.height = across, width, height
        self.frames = self.few * across
        self.block = (width + across - 1) // across
        self.groups = self.rows // 2
        wide = self.block + 4
        while self.few * 2 * wide % 8:
            wide += 1
        self.wide = wide
        self.stride = 2 * wide
        self.unit = self.few * self.stride
        self.cols = self.block + 2
        self.wide_out = round_up(self.block, 8)
        self.whole_blocks = self.block * across == width


def pack_kernel(plan, video_ref, out_ref, padded, joined):
    lead = 8
    for k in range(plan.few):
        for r in range(plan.rows):
            slot = k * plan.rows + r
            padded[slot, :lead] = jnp.zeros((lead, plan.chans), F32)
            padded[slot, lead : lead + plan.width] = video_ref[k, r].astype(F32)
            tail = padded.shape[1] - lead - plan.width
            padded[slot, lead + plan.width :] = jnp.zeros((tail, plan.chans), F32)
    for t in range(plan.across):
        for g in range(plan.groups):
            slot = (t * plan.groups + g) % joined.shape[0]
            for k in range(plan.few):
                for i in range(2):
                    start = lead - 2 + t * plan.block
                    to = (k * 2 + i) * plan.wide
                    piece = padded[k * plan.rows + 2 * g + i, start : start + plan.wide]
                    joined[slot, to : to + plan.wide] = piece
            out_ref[t, g] = joined[slot].astype(BF16)


def unpack_kernel(plan, got_ref, out_ref, joined):
    for k in range(plan.few):
        for r in range(plan.rows):
            slot = k * plan.rows + r
            for t in range(plan.across):
                at = t * plan.block
                joined[slot, at : at + plan.wide_out] = got_ref[t, k, r].astype(F32)
            out_ref[k, r] = joined[slot, : plan.width].astype(BF16)


def build_pair_weight(dst, src):
    chans = src.shape[-1]
    zero = jnp.zeros((chans, chans), BF16)
    for e in range(3):
        for j in range(4):
            for lag in range(3):
                at = ((j % 2) * 3 + lag) * chans
                for k in range(2):
                    tap = src[2 - lag, j - k, e] if 0 <= j - k <= 2 else zero
                    dst[e, j // 2, at : at + chans, k * chans : (k + 1) * chans] = tap


def act_taps(plan, x, gain, act, dst, g):
    guard = 2 * plan.stride
    act[:guard] = jnp.zeros((guard, plan.chans), F32)
    act[guard:] = silu(rms(x, gain))
    for i in range(2):
        for c in range(plan.block + 4):
            for lag in range(3):
                start = i * plan.wide + c + (2 - lag) * plan.stride
                v = act[pl.ds(start, plan.frames, stride=plan.stride), :]
                at = (i * 3 + lag) * plan.chans
                dst[g, c, :, at : at + plan.chans] = v.astype(BF16)


def half_conv(plan, field, g, weight, half, cols, total=None):
    for e in range(3):
        lhs = field[g, e : e + cols].reshape(cols * plan.frames, field.shape[-1])
        term = jnp.dot(lhs, weight[e, half], preferred_element_type=F32)
        total = term if total is None else total + term
    return total


def mid_taps(plan, total, p, hold, dst, g):
    frames, chans = plan.frames, plan.chans
    first_col = lax.axis_index("tm") * plan.block
    first_row = lax.axis_index("rows") * plan.rows
    mid = silu(total)
    for c in range(plan.cols):
        col = first_col + (c - 1)
        for k in range(2):
            row = first_row + (2 * p + k - 1)
            v = mid[c * frames : (c + 1) * frames, k * chans : (k + 1) * chans]
            edge_col = c in (0, plan.cols - 1) or not plan.whole_blocks
            edge_row = (p == 0 and k == 0) or (p == plan.groups and k == 1)
            if edge_col:
                v = jnp.where((col >= 0) & (col < plan.width), v, 0.0)
            if edge_row:
                v = jnp.where((row >= 0) & (row < plan.height), v, 0.0)
            hold[c, k, :8] = jnp.zeros((8, chans), F32)
            hold[c, k, 8:] = v
            for lag in range(3):
                moved = v if lag == 0 else hold[c, k, 8 - lag : 8 - lag + frames]
                at = (k * 3 + lag) * chans
                dst[g, c, :, at : at + chans] = moved.astype(BF16)


def first_kernel(
    plan,
    own_ref,
    gain_ref,
    k1_ref,
    k2_ref,
    pw1,
    pw2,
    part_ref,
    mid_ref,
    kept_ref,
    taps,
    act,
    raw,
    hold,
):
    gain = gain_ref[...].astype(F32)
    build_pair_weight(pw1, k1_ref)
    for g in range(plan.groups):
        x = own_ref[:, g].astype(F32).reshape(plan.across * plan.unit, plan.chans)
        raw[g] = x
        act_taps(plan, x, gain, act.at[g], taps, g)
        for i in range(2):
            for c in range(plan.block):
                start = i * plan.wide + c + 2
                v = raw[g, pl.ds(start, plan.frames, stride=plan.stride), :]
                kept_ref[2 * g + i, c] = v.astype(BF16)
    part_ref[0] = half_conv(plan, taps, 0, pw1, 1, plan.cols)
    for p in range(1, plan.groups):
        total = half_conv(plan, taps, p - 1, pw1, 0, plan.cols)
        total = half_conv(plan, taps, p, pw1, 1, plan.cols, total)
        mid_taps(plan, total, p, hold, mid_ref, p - 1)
    part_ref[1] = half_conv(plan, taps, plan.groups - 1, pw1, 0, plan.cols)
    build_pair_weight(pw2, k2_ref)


def second_kernel(
    plan,
    above_ref,
    below_ref,
    gain1_ref,
    pw1,
    pw2,
    part_ref,
    mid_ref,
    kept_ref,
    gain2_ref,
    wqkv_ref,
    wo_ref,
    out_ref,
    taps,
    act,
    mid,
    hold,
    hid,
    qkv,
    back,
):
    frames, rows, block, chans = plan.frames, plan.rows, plan.block, plan.chans
    gain1 = gain1_ref[...].astype(F32)
    gain2 = gain2_ref[...].astype(F32)

    totals = []
    for side, ref in enumerate((above_ref, below_ref)):
        x = ref[...].astype(F32).reshape(plan.across * plan.unit, chans)
        act_taps(plan, x, gain1, act.at[side], taps, side)
    for side in range(2):
        totals.append(half_conv(plan, taps, side, pw1, side, plan.cols, part_ref[side]))
    for side in range(2):
        mid_taps(plan, totals[side], side * plan.groups, hold.at[side], mid, side)

    def mid_group(g):
        if g == 0:
            return mid, 0
        return (mid, 1) if g == plan.groups else (mid_ref, g - 1)

    for q in range(plan.groups):
        total = half_conv(plan, *mid_group(q), pw2, 0, block)
        total = half_conv(plan, *mid_group(q + 1), pw2, 1, block, total)
        for k in range(2):
            r = 2 * q + k
            video = kept_ref[r].astype(F32).reshape(block * frames, chans)
            v = video + total[:, k * chans : (k + 1) * chans]
            hid[r * block * frames : (r + 1) * block * frames, :] = v.astype(BF16)

    count = rows * block * frames
    step = max(128 // frames, 1) * frames
    spans = [(lo, min(step, count - lo)) for lo in range(0, count, step)]
    scale = 1.0 / (float(chans) ** 0.5)
    for lo, n in spans:
        normed = rms(hid[lo : lo + n, :].astype(F32), gain2).astype(BF16)
        joined = jnp.dot(normed, wqkv_ref[...], preferred_element_type=F32)
        qkv[lo : lo + n, :] = joined.astype(BF16)
    i = lax.broadcasted_iota(jnp.int32, (step, step), 0)
    j = lax.broadcasted_iota(jnp.int32, (step, step), 1)
    allowed = (j <= i) & (j >= i - lax.rem(i, frames))
    scores = []
    for lo, n in spans:
        score = lax.dot_general(
            qkv[lo : lo + n, :chans],
            qkv[lo : lo + n, chans : 2 * chans],
            (((1,), (1,)), ((), ())),
            preferred_element_type=F32,
        )
        scores.append(jnp.where(allowed[:n, :n], score * scale, -1e30))
    weights = []
    for score in scores:
        top = jnp.max(score, axis=-1, keepdims=True)
        terms = jnp.exp(score - top)
        weights.append((terms.astype(BF16), jnp.sum(terms, axis=-1, keepdims=True)))
    results = []
    for (lo, n), (terms, total) in zip(spans, weights):
        values = qkv[lo : lo + n, 2 * chans :]
        mixed = jnp.dot(terms, values, preferred_element_type=F32) / total
        results.append(mixed.astype(BF16))
    for (lo, n), mixed in zip(spans, results):
        out = jnp.dot(mixed, wo_ref[...], preferred_element_type=F32)
        out = hid[lo : lo + n, :].astype(F32) + out
        for s in range(n // frames):
            r, c = divmod(lo // frames + s, block)
            back[r, pl.ds(c, frames, stride=plan.wide_out), :] = out[s * frames : (s + 1) * frames]

    for r in range(rows):
        out_ref[:, r] = back[r].reshape(frames, plan.wide_out, chans).astype(BF16)


def call(kernel, plan, outs, scratch, operands, name, flops, limit):
    shapes = [jax.ShapeDtypeStruct(s, d) for s, d in outs]
    moved = sum(s.size * s.dtype.itemsize for s in shapes)
    moved += sum(o.size * o.dtype.itemsize for o in operands)
    single = len(shapes) == 1
    return pl.pallas_call(
        functools.partial(kernel, plan),
        out_shape=shapes[0] if single else shapes,
        in_specs=[VMEM] * len(operands),
        out_specs=VMEM if single else [VMEM] * len(shapes),
        scratch_shapes=[pltpu.VMEM(s, d) for s, d in scratch],
        compiler_params=pltpu.CompilerParams(vmem_limit_bytes=limit),
        cost_estimate=pl.CostEstimate(flops=flops, bytes_accessed=moved, transcendentals=0),
        name=name,
    )(*operands)


def local(
    width,
    height,
    video,
    norm_gain,
    conv_first,
    conv_second,
    attn_gain,
    query_weight,
    key_weight,
    value_weight,
    out_weight,
):
    plan = Plan(video, lax.axis_size("tm"), width, height)
    down = lax.axis_size("rows")
    few, rows, groups, chans = plan.few, plan.rows, plan.groups, plan.chans
    across, frames, block, cols = plan.across, plan.frames, plan.block, plan.cols
    gain1 = norm_gain.reshape(1, chans)
    gain2 = attn_gain.reshape(1, chans)

    length = 8 + (across - 1) * block + plan.wide
    sent = call(
        pack_kernel,
        plan,
        [((across, groups, plan.unit, chans), BF16)],
        [((few * rows, round_up(max(length, 8 + width + 8), 8), chans), F32), ((4, plan.unit, chans), F32)],
        (video,),
        "pack",
        0,
        8 << 20,
    )
    own = lax.all_to_all(sent, "tm", 0, 0, tiled=True)

    above = lax.ppermute(own[:, groups - 1], "rows", [(i, i + 1) for i in range(down - 1)])
    below = lax.ppermute(own[:, 0], "rows", [(i + 1, i) for i in range(down - 1)])

    pair = (3, 2, 6 * chans, 2 * chans)
    guarded = (plan.frames + 2) * plan.stride
    pair_flops = 2 * 3 * cols * frames * 6 * chans * 2 * chans
    pw1, pw2, part, inner, kept = call(
        first_kernel,
        plan,
        [
            (pair, BF16),
            (pair, BF16),
            ((2, cols * frames, 2 * chans), F32),
            ((max(groups - 1, 1), cols, frames, 6 * chans), BF16),
            ((rows, block, frames, chans), BF16),
        ],
        [
            ((groups, block + 4, frames, 6 * chans), BF16),
            ((groups, guarded, chans), F32),
            ((groups, across * plan.unit, chans), F32),
            ((cols, 2, frames + 8, chans), F32),
        ],
        (own, gain1, conv_first, conv_second),
        "first",
        pair_flops * 2 * groups,
        24 << 20,
    )

    wqkv = jnp.concatenate([query_weight, key_weight, value_weight], axis=1)
    count = rows * block * frames
    out = call(
        second_kernel,
        plan,
        [((frames, rows, plan.wide_out, chans), BF16)],
        [
            ((2, block + 4, frames, 6 * chans), BF16),
            ((2, guarded, chans), F32),
            ((2, cols, frames, 6 * chans), BF16),
            ((2, cols, 2, frames + 8, chans), F32),
            ((count, chans), BF16),
            ((count, 3 * chans), BF16),
            ((rows, frames * plan.wide_out, chans), F32),
        ],
        (above, below, gain1, pw1, pw2, part, inner, kept, gain2, wqkv, out_weight),
        "second",
        pair_flops * 2 * (groups + 1),
        24 << 20,
    )

    sent = out.reshape(across, few, rows, plan.wide_out, chans)
    got = lax.all_to_all(sent, "tm", 0, 0, tiled=True)
    length = round_up(max((across - 1) * block + plan.wide_out, width), 8)
    return call(
        unpack_kernel,
        plan,
        [((few, rows, width, chans), BF16)],
        [((few * rows, length, chans), F32)],
        (got,),
        "unpack",
        0,
        8 << 20,
    )


def solution(mesh):
    spec = P("tm", "rows", None, None)

    def whole(video, *params):
        fn = functools.partial(local, video.shape[2], video.shape[1])
        return jax.shard_map(
            fn, mesh=mesh, in_specs=(spec,) + (P(),) * 8, out_specs=spec, check_vma=False
        )(video, *params)

    return whole
```

```python
import functools

import jax
import jax.numpy as jnp
from jax import lax
from jax.experimental import pallas as pl
from jax.experimental.pallas import tpu as pltpu
from jax.sharding import PartitionSpec as P

F32 = jnp.float32
BF16 = jnp.bfloat16
EPS = 1e-06
VMEM = pl.BlockSpec(memory_space=pltpu.VMEM)


def round_up(n, m):
    return (n + m - 1) // m * m


def silu(v):
    half = 0.5 * v
    return half + half * jnp.tanh(half)


def rms(v, gain):
    scale = lax.rsqrt(jnp.mean(v * v, axis=-1, keepdims=True) + EPS)
    return v * scale * gain


class Plan:
    def __init__(self, video, across, width, height):
        self.few, self.rows, _, self.chans = video.shape
        self.across, self.width, self.height = across, width, height
        self.frames = self.few * across
        self.block = (width + across - 1) // across
        self.groups = self.rows // 2
        self.chips = across // 2
        wide = self.block + 4
        while self.few * 2 * wide % 8:
            wide += 1
        self.wide = wide
        self.stride = 2 * wide
        self.unit = self.few * self.stride
        self.cols = self.block + 2
        self.wide_out = round_up(self.block, 8)
        self.whole_blocks = self.block * across == width


def pack_kernel(plan, s, video_ref, *refs):
    outs, (padded, joined) = refs[-plan.chips - 2 : -2], refs[-2:]
    lead = 8
    me = lax.axis_index("tm")
    for k in range(plan.few):
        for r in range(plan.rows):
            slot = k * plan.rows + r
            padded[slot, :lead] = jnp.zeros((lead, plan.chans), F32)
            padded[slot, lead : lead + plan.width] = video_ref[k, r].astype(F32)
            tail = padded.shape[1] - lead - plan.width
            padded[slot, lead + plan.width :] = jnp.zeros((tail, plan.chans), F32)
    for d in range(plan.chips):
        start = lead - 2 + jnp.bitwise_xor(me, 2 * d) * plan.block
        for g in range(plan.groups):
            at = (d * plan.groups + g) % joined.shape[0]
            for k in range(plan.few):
                for i in range(2):
                    slot = k * plan.rows + 2 * g + i
                    to = (k * 2 + i) * plan.wide
                    joined[at, to : to + plan.wide] = padded[slot, pl.ds(start, plan.wide)]
            outs[d][g, s] = joined[at].astype(BF16)


def unpack_kernel(plan, *refs):
    gots, rec_ref, out_ref, joined = refs[: plan.chips], *refs[plan.chips :]
    me = lax.axis_index("tm")
    for k in range(plan.few):
        for r in range(plan.rows):
            slot = k * plan.rows + r
            for d in range(plan.chips):
                for s in range(2):
                    at = jnp.bitwise_xor(me, 2 * d + s) * plan.block
                    part = rec_ref[d, k, r] if s else gots[d][0, k, r]
                    joined[slot, pl.ds(at, plan.block)] = part.astype(F32)[: plan.block]
            out_ref[k, r] = joined[slot, : plan.width].astype(BF16)


def prep_kernel(plan, *refs):
    sources, (pw1, pw2, wqkv, k1, k2, sems) = refs[:5], refs[5:]
    chans = plan.chans
    targets = [k1, k2] + [wqkv.at[:, i * chans : (i + 1) * chans] for i in range(3)]
    copies = []
    for i, (source, target) in enumerate(zip(sources, targets)):
        copies.append(pltpu.make_async_copy(source, target, sems.at[i]))
        copies[i].start()
    copies[0].wait()
    build_pair_weight(pw1, k1)
    copies[1].wait()
    build_pair_weight(pw2, k2)
    for copy in copies[2:]:
        copy.wait()


def build_pair_weight(dst, src):
    chans = src.shape[-1]
    zero = jnp.zeros((chans, chans), BF16)
    for e in range(3):
        for j in range(4):
            for lag in range(3):
                at = ((j % 2) * 3 + lag) * chans
                for k in range(2):
                    tap = src[2 - lag, j - k, e] if 0 <= j - k <= 2 else zero
                    dst[e, j // 2, at : at + chans, k * chans : (k + 1) * chans] = tap


def act_taps(plan, x, gain, act, dst, g):
    guard = 2 * plan.stride
    act[:guard] = jnp.zeros((guard, plan.chans), F32)
    act[guard:] = silu(rms(x, gain))
    for i in range(2):
        for c in range(plan.block + 4):
            for lag in range(3):
                start = i * plan.wide + c + (2 - lag) * plan.stride
                v = act[pl.ds(start, plan.frames, stride=plan.stride), :]
                at = (i * 3 + lag) * plan.chans
                dst[g, c, :, at : at + plan.chans] = v.astype(BF16)


def in_order(plan, pieces, raw):
    me = lax.axis_index("tm")
    for i in range(plan.across):
        to = pl.multiple_of(jnp.bitwise_xor(me, i) * plan.unit, 8)
        raw[pl.ds(to, plan.unit), :] = pieces(i).astype(F32)


def half_conv(plan, parts, weight, half, cols, total=None):
    for e in range(3):
        lhs = [
            f[g : g + n, e : e + cols].reshape(n * cols * plan.frames, f.shape[-1])
            for f, g, n in parts
        ]
        lhs = lhs[0] if len(lhs) == 1 else jnp.concatenate(lhs, axis=0)
        term = jnp.dot(lhs, weight[e, half], preferred_element_type=F32)
        total = term if total is None else total + term
    return total


def mid_taps(plan, total, p, hold, dst, g):
    frames, chans = plan.frames, plan.chans
    first_col = lax.axis_index("tm") * plan.block
    first_row = lax.axis_index("rows") * plan.rows
    mid = silu(total)
    for c in range(plan.cols):
        col = first_col + (c - 1)
        for k in range(2):
            row = first_row + (2 * p + k - 1)
            v = mid[c * frames : (c + 1) * frames, k * chans : (k + 1) * chans]
            edge_col = c in (0, plan.cols - 1) or not plan.whole_blocks
            edge_row = (p == 0 and k == 0) or (p == plan.groups and k == 1)
            if edge_col:
                v = jnp.where((col >= 0) & (col < plan.width), v, 0.0)
            if edge_row:
                v = jnp.where((row >= 0) & (row < plan.height), v, 0.0)
            hold[c, k, :8] = jnp.zeros((8, chans), F32)
            hold[c, k, 8:] = v
            for lag in range(3):
                moved = v if lag == 0 else hold[c, k, 8 - lag : 8 - lag + frames]
                at = (k * 3 + lag) * chans
                dst[g, c, :, at : at + chans] = moved.astype(BF16)


def first_kernel(plan, *refs):
    pieces, refs = refs[: plan.chips], refs[plan.chips :]
    gain_ref, pw1, part_ref, mid_ref, kept_ref, taps, act, raw, hold = refs
    gain = gain_ref[...].astype(F32)
    for g in range(plan.groups):
        in_order(plan, lambda i: pieces[i // 2][g, i % 2], raw.at[g])
        act_taps(plan, raw[g], gain, act.at[g], taps, g)
        for i in range(2):
            for c in range(plan.block):
                start = i * plan.wide + c + 2
                v = raw[g, pl.ds(start, plan.frames, stride=plan.stride), :]
                kept_ref[2 * g + i, c] = v.astype(BF16)
    lower = half_conv(plan, [(taps, 0, plan.groups)], pw1, 0, plan.cols)
    upper = half_conv(plan, [(taps, 0, plan.groups)], pw1, 1, plan.cols)
    size = plan.cols * plan.frames
    part_ref[0] = upper[:size]
    for p in range(1, plan.groups):
        total = lower[(p - 1) * size : p * size] + upper[p * size : (p + 1) * size]
        mid_taps(plan, total, p, hold, mid_ref, p - 1)
    part_ref[1] = lower[(plan.groups - 1) * size :]


def second_kernel(plan, *refs):
    sides, refs = refs[:2], refs[2:]
    gain1_ref, pw1, pw2, part_ref, mid_ref, kept_ref, gain2_ref, wqkv_ref, wo_ref = refs[:9]
    outs, refs = refs[9 : 9 + plan.chips], refs[9 + plan.chips :]
    taps, act, raw, mid, hold, hid, qkv, back = refs
    frames, rows, block, chans = plan.frames, plan.rows, plan.block, plan.chans
    gain1 = gain1_ref[...].astype(F32)
    gain2 = gain2_ref[...].astype(F32)

    totals = []
    for side, ref in enumerate(sides):
        in_order(plan, lambda i: ref[i], raw.at[side])
        act_taps(plan, raw[side], gain1, act.at[side], taps, side)
    for side in range(2):
        total = half_conv(plan, [(taps, side, 1)], pw1, side, plan.cols)
        totals.append(total + part_ref[side])
    for side in range(2):
        mid_taps(plan, totals[side], side * plan.groups, hold.at[side], mid, side)

    def mid_group(g):
        if g == 0:
            return [(mid, 0, 1)]
        return [(mid, 1, 1)] if g == plan.groups else [(mid_ref, g - 1, 1)]

    size = block * frames
    for q in range(plan.groups):
        total = half_conv(plan, mid_group(q), pw2, 0, block)
        total = half_conv(plan, mid_group(q + 1), pw2, 1, block, total)
        for k in range(2):
            r = 2 * q + k
            video = kept_ref[r].astype(F32).reshape(size, chans)
            v = video + total[:, k * chans : (k + 1) * chans]
            hid[r * size : (r + 1) * size, :] = v.astype(BF16)

    count = rows * size
    step = max(128 // frames, 1) * frames
    spans = [(lo, min(step, count - lo)) for lo in range(0, count, step)]
    scale = 1.0 / (float(chans) ** 0.5)
    for lo, n in spans:
        normed = rms(hid[lo : lo + n, :].astype(F32), gain2).astype(BF16)
        joined = jnp.dot(normed, wqkv_ref[...], preferred_element_type=F32)
        qkv[lo : lo + n, :] = joined.astype(BF16)
    i = lax.broadcasted_iota(jnp.int32, (step, step), 0)
    j = lax.broadcasted_iota(jnp.int32, (step, step), 1)
    allowed = (j <= i) & (j >= i - lax.rem(i, frames))
    scores = []
    for lo, n in spans:
        score = lax.dot_general(
            qkv[lo : lo + n, :chans],
            qkv[lo : lo + n, chans : 2 * chans],
            (((1,), (1,)), ((), ())),
            preferred_element_type=F32,
        )
        scores.append(jnp.where(allowed[:n, :n], score * scale, -1e30))
    weights = []
    for score in scores:
        top = jnp.max(score, axis=-1, keepdims=True)
        terms = jnp.exp(score - top)
        weights.append((terms.astype(BF16), jnp.sum(terms, axis=-1, keepdims=True)))
    results = []
    for (lo, n), (terms, total) in zip(spans, weights):
        values = qkv[lo : lo + n, 2 * chans :]
        mixed = jnp.dot(terms, values, preferred_element_type=F32) / total
        results.append(mixed.astype(BF16))
    for (lo, n), mixed in zip(spans, results):
        out = jnp.dot(mixed, wo_ref[...], preferred_element_type=F32)
        out = hid[lo : lo + n, :].astype(F32) + out
        for s in range(n // frames):
            r, c = divmod(lo // frames + s, block)
            v = out[s * frames : (s + 1) * frames]
            back[r, pl.ds(c, frames, stride=plan.wide_out), :] = v

    me = lax.axis_index("tm")
    for d in range(plan.chips):
        for s in range(2):
            owner = jnp.bitwise_xor(me, 2 * d + s)
            span = plan.few * plan.wide_out
            for r in range(rows):
                v = back[r, pl.ds(pl.multiple_of(owner * span, 8), span), :]
                v = v.reshape(plan.few, plan.wide_out, chans)
                outs[d][s, :, r] = v.astype(BF16)


def call(kernel, outs, scratch, operands, name, flops, limit, specs=None, aliases=None):
    shapes = [jax.ShapeDtypeStruct(s, d) for s, d in outs]
    moved = sum(s.size * s.dtype.itemsize for s in shapes) if flops else 0
    single = len(shapes) == 1
    scratch = [pltpu.VMEM(*s) if isinstance(s, tuple) else s for s in scratch]
    return pl.pallas_call(
        kernel,
        out_shape=shapes[0] if single else shapes,
        in_specs=specs or [VMEM] * len(operands),
        out_specs=VMEM if single else [VMEM] * len(shapes),
        scratch_shapes=scratch,
        input_output_aliases=aliases or {},
        compiler_params=pltpu.CompilerParams(vmem_limit_bytes=limit),
        cost_estimate=pl.CostEstimate(flops=flops, bytes_accessed=moved, transcendentals=0),
        name=name,
    )(*operands)


def exchange(value, distance):
    size = lax.axis_size("tm")
    return lax.ppermute(value, "tm", [(i, i ^ distance) for i in range(size)])


def local(
    width,
    height,
    video,
    norm_gain,
    conv_first,
    conv_second,
    attn_gain,
    query_weight,
    key_weight,
    value_weight,
    out_weight,
):
    plan = Plan(video, lax.axis_size("tm"), width, height)
    down = lax.axis_size("rows")
    few, rows, groups, chans = plan.few, plan.rows, plan.groups, plan.chans
    across, frames, block, cols = plan.across, plan.frames, plan.block, plan.cols
    chips, unit = plan.chips, plan.unit
    gain1 = norm_gain.reshape(1, chans)
    gain2 = attn_gain.reshape(1, chans)

    other = exchange(video, 1)
    length = round_up(max(8 + (across - 1) * block + plan.wide, 8 + width + 8), 8)
    pieces = ()
    for s, value in enumerate((video, other)):
        pieces = call(
            functools.partial(pack_kernel, plan, s),
            [((groups, 2, unit, chans), BF16)] * chips,
            [((few * rows, length, chans), F32), ((4, unit, chans), F32)],
            (value, *pieces),
            ("pack_own", "pack_other")[s],
            0,
            4 << 20,
            aliases={1 + d: d for d in range(chips)} if s else None,
            specs=[VMEM] + [pl.BlockSpec(memory_space=pl.ANY)] * (chips if s else 0),
        )
    pieces = [pieces[0]] + [exchange(pieces[d], 2 * d) for d in range(1, chips)]

    pair = (3, 2, 6 * chans, 2 * chans)
    pair_flops = 2 * 3 * cols * frames * 6 * chans * 2 * chans
    prepared = call(
        functools.partial(prep_kernel, plan),
        [(pair, BF16), (pair, BF16), ((chans, 3 * chans), BF16)],
        [(conv_first.shape, BF16), (conv_second.shape, BF16), pltpu.SemaphoreType.DMA((5,))],
        [
            pltpu.with_memory_space_constraint(w, pltpu.HBM)
            for w in (conv_first, conv_second, query_weight, key_weight, value_weight)
        ],
        "prep",
        0,
        4 << 20,
        specs=[pl.BlockSpec(memory_space=pltpu.HBM)] * 5,
    )
    pieces, (pw1, pw2, wqkv) = lax.optimization_barrier((pieces, prepared))

    upward = jnp.concatenate([p[groups - 1] for p in pieces])
    downward = jnp.concatenate([p[0] for p in pieces])
    above = lax.ppermute(upward, "rows", [(i, i + 1) for i in range(down - 1)])
    below = lax.ppermute(downward, "rows", [(i + 1, i) for i in range(down - 1)])

    guarded = (frames + 2) * plan.stride
    part, inner, kept = call(
        functools.partial(first_kernel, plan),
        [
            ((2, cols * frames, 2 * chans), F32),
            ((max(groups - 1, 1), cols, frames, 6 * chans), BF16),
            ((rows, block, frames, chans), BF16),
        ],
        [
            ((groups, block + 4, frames, 6 * chans), BF16),
            ((groups, guarded, chans), F32),
            ((groups, across * unit, chans), F32),
            ((cols, 2, frames + 8, chans), F32),
        ],
        (*pieces, gain1, pw1),
        "first",
        pair_flops * 2 * groups,
        24 << 20,
    )

    count = rows * block * frames
    outs = call(
        functools.partial(second_kernel, plan),
        [((2, few, rows, plan.wide_out, chans), BF16)] * chips,
        [
            ((2, block + 4, frames, 6 * chans), BF16),
            ((2, guarded, chans), F32),
            ((2, across * unit, chans), F32),
            ((2, cols, frames, 6 * chans), BF16),
            ((2, cols, 2, frames + 8, chans), F32),
            ((count, chans), BF16),
            ((count, 3 * chans), BF16),
            ((rows, frames * plan.wide_out, chans), F32),
        ],
        (above, below, gain1, pw1, pw2, part, inner, kept, gain2, wqkv, out_weight),
        "second",
        pair_flops * 2 * (groups + 1),
        24 << 20,
    )

    gots = [outs[0]] + [exchange(outs[d], 2 * d) for d in range(1, chips)]
    rec = exchange(jnp.stack([g[1] for g in gots]), 1)
    length = round_up(max(across * block, width), 8)
    return call(
        functools.partial(unpack_kernel, plan),
        [((few, rows, width, chans), BF16)],
        [((few * rows, length, chans), F32)],
        (*gots, rec),
        "unpack",
        0,
        8 << 20,
    )


def solution(mesh):
    spec = P("tm", "rows", None, None)

    def whole(video, *params):
        fn = functools.partial(local, video.shape[2], video.shape[1])
        return jax.shard_map(
            fn, mesh=mesh, in_specs=(spec,) + (P(),) * 8, out_specs=spec, check_vma=False
        )(video, *params)

    return whole
```

```python
import functools

import jax
import jax.numpy as jnp
from jax import lax
from jax.experimental import pallas as pl
from jax.experimental.pallas import tpu as pltpu
from jax.sharding import PartitionSpec as P

F32 = jnp.float32
BF16 = jnp.bfloat16
EPS = 1e-06
VMEM = pl.BlockSpec(memory_space=pltpu.VMEM)


def round_up(n, m):
    return (n + m - 1) // m * m


def silu(v):
    half = 0.5 * v
    return half + half * jnp.tanh(half)


def rms(v, gain):
    scale = lax.rsqrt(jnp.mean(v * v, axis=-1, keepdims=True) + EPS)
    return v * scale * gain


class Plan:
    def __init__(self, video, across, width, height):
        self.few, self.rows, _, self.chans = video.shape
        self.across, self.width, self.height = across, width, height
        self.frames = self.few * across
        self.block = (width + across - 1) // across
        self.groups = self.rows // 2
        self.chips = across // 2
        wide = self.block + 4
        while self.few * 2 * wide % 8:
            wide += 1
        self.wide = wide
        self.stride = 2 * wide
        self.unit = self.few * self.stride
        self.cols = self.block + 2
        self.wide_out = round_up(self.block, 8)
        self.whole_blocks = self.block * across == width


def pack_kernel(plan, s, video_ref, *refs):
    outs, (padded, joined) = refs[-plan.chips - 2 : -2], refs[-2:]
    lead = 8
    me = lax.axis_index("tm")
    for k in range(plan.few):
        for r in range(plan.rows):
            slot = k * plan.rows + r
            padded[slot, :lead] = jnp.zeros((lead, plan.chans), F32)
            padded[slot, lead : lead + plan.width] = video_ref[k, r].astype(F32)
            tail = padded.shape[1] - lead - plan.width
            padded[slot, lead + plan.width :] = jnp.zeros((tail, plan.chans), F32)
    for d in range(plan.chips):
        start = lead - 2 + jnp.bitwise_xor(me, 2 * d) * plan.block
        for g in range(plan.groups):
            at = (d * plan.groups + g) % joined.shape[0]
            for k in range(plan.few):
                for i in range(2):
                    slot = k * plan.rows + 2 * g + i
                    to = (k * 2 + i) * plan.wide
                    joined[at, to : to + plan.wide] = padded[slot, pl.ds(start, plan.wide)]
            outs[d][g, s] = joined[at].astype(BF16)


def unpack_kernel(plan, *refs):
    gots, rec_ref, out_ref, joined = refs[: plan.chips], *refs[plan.chips :]
    me = lax.axis_index("tm")
    for k in range(plan.few):
        for r in range(plan.rows):
            slot = k * plan.rows + r
            for d in range(plan.chips):
                for s in range(2):
                    at = jnp.bitwise_xor(me, 2 * d + s) * plan.block
                    part = rec_ref[d, k, r] if s else gots[d][0, k, r]
                    joined[slot, pl.ds(at, plan.block)] = part.astype(F32)[: plan.block]
            out_ref[k, r] = joined[slot, : plan.width].astype(BF16)


def prep_kernel(plan, *refs):
    sources, (pw1, pw2, wqkv, k1, k2, sems) = refs[:5], refs[5:]
    chans = plan.chans
    targets = [k1, k2] + [wqkv.at[:, i * chans : (i + 1) * chans] for i in range(3)]
    copies = []
    for i, (source, target) in enumerate(zip(sources, targets)):
        copies.append(pltpu.make_async_copy(source, target, sems.at[i]))
        copies[i].start()
    copies[0].wait()
    build_pair_weight(pw1, k1)
    copies[1].wait()
    build_pair_weight(pw2, k2)
    for copy in copies[2:]:
        copy.wait()


def build_pair_weight(dst, src):
    chans = src.shape[-1]
    zero = jnp.zeros((chans, chans), BF16)
    for e in range(3):
        for j in range(4):
            for lag in range(3):
                at = ((j % 2) * 3 + lag) * chans
                for k in range(2):
                    tap = src[2 - lag, j - k, e] if 0 <= j - k <= 2 else zero
                    dst[e, j // 2, at : at + chans, k * chans : (k + 1) * chans] = tap


def act_taps(plan, x, gain, act, dst, g):
    guard = 2 * plan.stride
    act[:guard] = jnp.zeros((guard, plan.chans), F32)
    act[guard:] = silu(rms(x, gain))
    for i in range(2):
        for c in range(plan.block + 4):
            for lag in range(3):
                start = i * plan.wide + c + (2 - lag) * plan.stride
                v = act[pl.ds(start, plan.frames, stride=plan.stride), :]
                at = (i * 3 + lag) * plan.chans
                dst[g, c, :, at : at + plan.chans] = v.astype(BF16)


def in_order(plan, pieces, raw):
    me = lax.axis_index("tm")
    for i in range(plan.across):
        to = pl.multiple_of(jnp.bitwise_xor(me, i) * plan.unit, 8)
        raw[pl.ds(to, plan.unit), :] = pieces(i).astype(F32)


def half_conv(plan, parts, weight, half, cols, total=None):
    for e in range(3):
        lhs = [
            f[g : g + n, e : e + cols].reshape(n * cols * plan.frames, f.shape[-1])
            for f, g, n in parts
        ]
        lhs = lhs[0] if len(lhs) == 1 else jnp.concatenate(lhs, axis=0)
        term = jnp.dot(lhs, weight[e, half], preferred_element_type=F32)
        total = term if total is None else total + term
    return total


def mid_taps(plan, total, p, hold, dst, g):
    frames, chans = plan.frames, plan.chans
    first_col = lax.axis_index("tm") * plan.block
    first_row = lax.axis_index("rows") * plan.rows
    mid = silu(total)
    for c in range(plan.cols):
        col = first_col + (c - 1)
        for k in range(2):
            row = first_row + (2 * p + k - 1)
            v = mid[c * frames : (c + 1) * frames, k * chans : (k + 1) * chans]
            edge_col = c in (0, plan.cols - 1) or not plan.whole_blocks
            edge_row = (p == 0 and k == 0) or (p == plan.groups and k == 1)
            if edge_col:
                v = jnp.where((col >= 0) & (col < plan.width), v, 0.0)
            if edge_row:
                v = jnp.where((row >= 0) & (row < plan.height), v, 0.0)
            hold[c, k, :8] = jnp.zeros((8, chans), F32)
            hold[c, k, 8:] = v
            for lag in range(3):
                moved = v if lag == 0 else hold[c, k, 8 - lag : 8 - lag + frames]
                at = (k * 3 + lag) * chans
                dst[g, c, :, at : at + chans] = moved.astype(BF16)


def first_kernel(plan, *refs):
    pieces, refs = refs[: plan.chips], refs[plan.chips :]
    gain_ref, pw1, part_ref, mid_ref, kept_ref, taps, act, raw, hold = refs
    gain = gain_ref[...].astype(F32)
    for g in range(plan.groups):
        in_order(plan, lambda i: pieces[i // 2][g, i % 2], raw.at[g])
        act_taps(plan, raw[g], gain, act.at[g], taps, g)
        for i in range(2):
            for c in range(plan.block):
                start = i * plan.wide + c + 2
                v = raw[g, pl.ds(start, plan.frames, stride=plan.stride), :]
                kept_ref[2 * g + i, c] = v.astype(BF16)
    lower = half_conv(plan, [(taps, 0, plan.groups)], pw1, 0, plan.cols)
    upper = half_conv(plan, [(taps, 0, plan.groups)], pw1, 1, plan.cols)
    size = plan.cols * plan.frames
    part_ref[0] = upper[:size]
    for p in range(1, plan.groups):
        total = lower[(p - 1) * size : p * size] + upper[p * size : (p + 1) * size]
        mid_taps(plan, total, p, hold, mid_ref, p - 1)
    part_ref[1] = lower[(plan.groups - 1) * size :]


def second_kernel(plan, *refs):
    swaps, refs = refs[:2], refs[2:]
    gain1_ref, pw1, pw2, part_ref, mid_ref, kept_ref, gain2_ref, wqkv_ref, wo_ref = refs[:9]
    outs, refs = refs[9 : 9 + plan.chips], refs[9 + plan.chips :]
    taps, act, raw, mid, hold, hid, qkv, back = refs
    frames, rows, block, chans = plan.frames, plan.rows, plan.block, plan.chans
    gain1 = gain1_ref[...].astype(F32)
    gain2 = gain2_ref[...].astype(F32)

    totals = []
    odd = lax.rem(lax.axis_index("rows"), 2)
    for order, ref in enumerate(swaps):
        side = odd if order == 0 else 1 - odd
        in_order(plan, lambda i: ref[i], raw.at[side])
    for side in range(2):
        act_taps(plan, raw[side], gain1, act.at[side], taps, side)
    for side in range(2):
        total = half_conv(plan, [(taps, side, 1)], pw1, side, plan.cols)
        totals.append(total + part_ref[side])
    for side in range(2):
        mid_taps(plan, totals[side], side * plan.groups, hold.at[side], mid, side)

    def mid_group(g):
        if g == 0:
            return [(mid, 0, 1)]
        return [(mid, 1, 1)] if g == plan.groups else [(mid_ref, g - 1, 1)]

    size = block * frames
    for q in range(plan.groups):
        total = half_conv(plan, mid_group(q), pw2, 0, block)
        total = half_conv(plan, mid_group(q + 1), pw2, 1, block, total)
        for k in range(2):
            r = 2 * q + k
            video = kept_ref[r].astype(F32).reshape(size, chans)
            v = video + total[:, k * chans : (k + 1) * chans]
            hid[r * size : (r + 1) * size, :] = v.astype(BF16)

    count = rows * size
    step = max(128 // frames, 1) * frames
    spans = [(lo, min(step, count - lo)) for lo in range(0, count, step)]
    scale = 1.0 / (float(chans) ** 0.5)
    for lo, n in spans:
        normed = rms(hid[lo : lo + n, :].astype(F32), gain2).astype(BF16)
        joined = jnp.dot(normed, wqkv_ref[...], preferred_element_type=F32)
        qkv[lo : lo + n, :] = joined.astype(BF16)
    i = lax.broadcasted_iota(jnp.int32, (step, step), 0)
    j = lax.broadcasted_iota(jnp.int32, (step, step), 1)
    allowed = (j <= i) & (j >= i - lax.rem(i, frames))
    scores = []
    for lo, n in spans:
        score = lax.dot_general(
            qkv[lo : lo + n, :chans],
            qkv[lo : lo + n, chans : 2 * chans],
            (((1,), (1,)), ((), ())),
            preferred_element_type=F32,
        )
        scores.append(jnp.where(allowed[:n, :n], score * scale, -1e30))
    weights = []
    for score in scores:
        top = jnp.max(score, axis=-1, keepdims=True)
        terms = jnp.exp(score - top)
        weights.append((terms.astype(BF16), jnp.sum(terms, axis=-1, keepdims=True)))
    results = []
    for (lo, n), (terms, total) in zip(spans, weights):
        values = qkv[lo : lo + n, 2 * chans :]
        mixed = jnp.dot(terms, values, preferred_element_type=F32) / total
        results.append(mixed.astype(BF16))
    for (lo, n), mixed in zip(spans, results):
        out = jnp.dot(mixed, wo_ref[...], preferred_element_type=F32)
        out = hid[lo : lo + n, :].astype(F32) + out
        for s in range(n // frames):
            r, c = divmod(lo // frames + s, block)
            v = out[s * frames : (s + 1) * frames]
            back[r, pl.ds(c, frames, stride=plan.wide_out), :] = v

    me = lax.axis_index("tm")
    for d in range(plan.chips):
        for s in range(2):
            owner = jnp.bitwise_xor(me, 2 * d + s)
            span = plan.few * plan.wide_out
            for r in range(rows):
                v = back[r, pl.ds(pl.multiple_of(owner * span, 8), span), :]
                v = v.reshape(plan.few, plan.wide_out, chans)
                outs[d][s, :, r] = v.astype(BF16)


def call(kernel, outs, scratch, operands, name, flops, limit, specs=None, aliases=None):
    shapes = [jax.ShapeDtypeStruct(s, d) for s, d in outs]
    moved = sum(s.size * s.dtype.itemsize for s in shapes) if flops else 0
    single = len(shapes) == 1
    scratch = [pltpu.VMEM(*s) if isinstance(s, tuple) else s for s in scratch]
    return pl.pallas_call(
        kernel,
        out_shape=shapes[0] if single else shapes,
        in_specs=specs or [VMEM] * len(operands),
        out_specs=VMEM if single else [VMEM] * len(shapes),
        scratch_shapes=scratch,
        input_output_aliases=aliases or {},
        compiler_params=pltpu.CompilerParams(vmem_limit_bytes=limit),
        cost_estimate=pl.CostEstimate(flops=flops, bytes_accessed=moved, transcendentals=0),
        name=name,
    )(*operands)


def exchange(value, distance):
    size = lax.axis_size("tm")
    return lax.ppermute(value, "tm", [(i, i ^ distance) for i in range(size)])


def local(
    width,
    height,
    video,
    norm_gain,
    conv_first,
    conv_second,
    attn_gain,
    query_weight,
    key_weight,
    value_weight,
    out_weight,
):
    plan = Plan(video, lax.axis_size("tm"), width, height)
    down = lax.axis_size("rows")
    few, rows, groups, chans = plan.few, plan.rows, plan.groups, plan.chans
    across, frames, block, cols = plan.across, plan.frames, plan.block, plan.cols
    chips, unit = plan.chips, plan.unit
    gain1 = norm_gain.reshape(1, chans)
    gain2 = attn_gain.reshape(1, chans)

    other = exchange(video, 1)
    length = round_up(max(8 + (across - 1) * block + plan.wide, 8 + width + 8), 8)
    pieces = ()
    for s, value in enumerate((video, other)):
        pieces = call(
            functools.partial(pack_kernel, plan, s),
            [((groups, 2, unit, chans), BF16)] * chips,
            [((few * rows, length, chans), F32), ((4, unit, chans), F32)],
            (value, *pieces),
            ("pack_own", "pack_other")[s],
            0,
            4 << 20,
            aliases={1 + d: d for d in range(chips)} if s else None,
            specs=[VMEM] + [pl.BlockSpec(memory_space=pl.ANY)] * (chips if s else 0),
        )
    pieces = [pieces[0]] + [exchange(pieces[d], 2 * d) for d in range(1, chips)]

    pair = (3, 2, 6 * chans, 2 * chans)
    pair_flops = 2 * 3 * cols * frames * 6 * chans * 2 * chans
    prepared = call(
        functools.partial(prep_kernel, plan),
        [(pair, BF16), (pair, BF16), ((chans, 3 * chans), BF16)],
        [(conv_first.shape, BF16), (conv_second.shape, BF16), pltpu.SemaphoreType.DMA((5,))],
        [
            pltpu.with_memory_space_constraint(w, pltpu.HBM)
            for w in (conv_first, conv_second, query_weight, key_weight, value_weight)
        ],
        "prep",
        0,
        4 << 20,
        specs=[pl.BlockSpec(memory_space=pltpu.HBM)] * 5,
    )
    pieces, (pw1, pw2, wqkv) = lax.optimization_barrier((pieces, prepared))

    even = lax.axis_index("rows") % 2 == 0
    upward = jnp.concatenate([p[groups - 1] for p in pieces])
    downward = jnp.concatenate([p[0] for p in pieces])
    swaps = []
    for offset in (1, 0):
        pairs = [(i, i + 1) for i in range(offset, down - 1, 2)]
        pairs = pairs + [(j, i) for i, j in pairs]
        ahead = even if offset == 0 else jnp.logical_not(even)
        swaps.append(lax.ppermute(jnp.where(ahead, upward, downward), "rows", pairs))

    guarded = (frames + 2) * plan.stride
    part, inner, kept = call(
        functools.partial(first_kernel, plan),
        [
            ((2, cols * frames, 2 * chans), F32),
            ((max(groups - 1, 1), cols, frames, 6 * chans), BF16),
            ((rows, block, frames, chans), BF16),
        ],
        [
            ((groups, block + 4, frames, 6 * chans), BF16),
            ((groups, guarded, chans), F32),
            ((groups, across * unit, chans), F32),
            ((cols, 2, frames + 8, chans), F32),
        ],
        (*pieces, gain1, pw1),
        "first",
        pair_flops * 2 * groups,
        24 << 20,
    )

    count = rows * block * frames
    outs = call(
        functools.partial(second_kernel, plan),
        [((2, few, rows, plan.wide_out, chans), BF16)] * chips,
        [
            ((2, block + 4, frames, 6 * chans), BF16),
            ((2, guarded, chans), F32),
            ((2, across * unit, chans), F32),
            ((2, cols, frames, 6 * chans), BF16),
            ((2, cols, 2, frames + 8, chans), F32),
            ((count, chans), BF16),
            ((count, 3 * chans), BF16),
            ((rows, frames * plan.wide_out, chans), F32),
        ],
        (*swaps, gain1, pw1, pw2, part, inner, kept, gain2, wqkv, out_weight),
        "second",
        pair_flops * 2 * (groups + 1),
        24 << 20,
    )

    gots = [outs[0]] + [exchange(outs[d], 2 * d) for d in range(1, chips)]
    rec = exchange(jnp.stack([g[1] for g in gots]), 1)
    length = round_up(max(across * block, width), 8)
    return call(
        functools.partial(unpack_kernel, plan),
        [((few, rows, width, chans), BF16)],
        [((few * rows, length, chans), F32)],
        (*gots, rec),
        "unpack",
        0,
        8 << 20,
    )


def solution(mesh):
    spec = P("tm", "rows", None, None)

    def whole(video, *params):
        fn = functools.partial(local, video.shape[2], video.shape[1])
        return jax.shard_map(
            fn, mesh=mesh, in_specs=(spec,) + (P(),) * 8, out_specs=spec, check_vma=False
        )(video, *params)

    return whole
```
